32 devices in a mesh: seq: 1, ctx: 8 (over y, x, core), head: 4 (over z).
Axes of the slice: x: 2, y: 2, z: 4, core: 2. Of those that a mesh axis runs over, the one named last changes fastest.
Arguments:
- queries: bfloat16 [3072, 4096], P(('seq', 'ctx'), 'head'), may hold values from -6 to 6
- keys: bfloat16 [3072, 4096], P(('seq', 'ctx'), 'head'), may hold values from -6 to 6
- values: bfloat16 [3072, 4096], P(('seq', 'ctx'), 'head'), may hold values from -6 to 6
- grad_out: bfloat16 [3072, 4096], P(('seq', 'ctx'), 'head'), may hold values from -6 to 6
Outputs:
- attn_out: bfloat16 [3072, 4096], P(('seq', 'ctx'), 'head')
- grad_queries: bfloat16 [3072, 4096], P(('seq', 'ctx'), 'head')
- grad_keys: bfloat16 [3072, 4096], P(('seq', 'ctx'), 'head')
- grad_values: bfloat16 [3072, 4096], P(('seq', 'ctx'), 'head')
The draws below stay inside these ranges and needn't reach their ends.
All inputs are finite; a program needn't handle non-finite values.
Results may differ from the reference program's by a relative error of at most 0.0051.
Values sent between devices are 32-bit elements; how exact they have to be, the bound alone decides.
A program may use at most 64 MiB of HBM per device.

```python
import jax
import jax.numpy as jnp
from jax import lax

HEADS = 32
DH = 128
TOK_DEV = 384
SEQ_LEN = 3072


def block_levels(own_key, dims, split, least, top_value):
    level, own = 1.0, jax.random.fold_in(own_key, 6)
    for dim, shards_of in split:
        draws = jnp.exp(jax.random.uniform(jax.random.fold_in(own, dim), (shards_of,), jnp.float32, least / len(split), top_value / len(split)))
        level = level * jnp.repeat(draws, dims[dim] // shards_of).reshape([-1 if axis == dim else 1 for axis in range(len(dims))])
    return level


def noise(rng, shape, width, reach, cuts=(), held_as=jnp.bfloat16):
    values = jax.random.normal(rng, shape, jnp.float32) * width
    if len(cuts) > 0:
        values = block_levels(rng, shape, cuts, -0.22, 0.18) * values
    return jnp.clip(values, min=-reach, max=reach).astype(held_as)


def setup_inputs(seed: int = 0, part: int = 0) -> dict:
    seeds = jax.random.split(jax.random.key(seed), 5)
    part_splits = jax.random.split(jax.random.fold_in(seeds[4], part), 5)
    queries = noise(part_splits[0], (SEQ_LEN, HEADS * DH), 1.0, 6.0, ((0, 8), (1, 4)))
    keys = noise(part_splits[1], (SEQ_LEN, HEADS * DH), 1.0, 6.0, ((0, 8), (1, 4)))
    values = noise(part_splits[2], (SEQ_LEN, HEADS * DH), 1.0, 6.0, ((0, 8), (1, 4)))
    grad_out = noise(part_splits[3], (SEQ_LEN, HEADS * DH), 1.0, 6.0, ((0, 8), (1, 4)))
    return dict(queries=queries, keys=keys, values=values, grad_out=grad_out)


def to_bf_and_back(array):
    rounded = lax.optimization_barrier(array.astype(jnp.bfloat16))
    return rounded.astype(jnp.float32)

def reference(queries, keys, values, grad_out):
    blocks = SEQ_LEN // TOK_DEV
    factor = 1.0 / jnp.sqrt(jnp.float32(DH * SEQ_LEN))

    def split_heads(array):
        return array.reshape(blocks, TOK_DEV, HEADS, DH).astype(jnp.float32)
    query_part = split_heads(queries)
    key_part = split_heads(keys)
    value_part = split_heads(values)
    grad_part = split_heads(grad_out)
    causal = jnp.tril(jnp.ones((TOK_DEV, TOK_DEV), jnp.float32))
    kv_local = jnp.einsum('bshd,bshe->bhde', key_part, value_part)
    zero_state = jnp.zeros((1,) + kv_local.shape[1:], jnp.float32)
    kv_prefix = jnp.concatenate([zero_state, jnp.cumsum(kv_local, axis=0)[:-1]], axis=0)
    kv_prefix = to_bf_and_back(kv_prefix)
    qg_local = jnp.einsum('bshd,bshe->bhde', query_part, grad_part)
    qg_rev = jnp.cumsum(qg_local[::-1], axis=0)[:-1]
    qg_suffix = jnp.concatenate([zero_state, qg_rev], axis=0)[::-1]
    qg_suffix = to_bf_and_back(qg_suffix)
    scores = to_bf_and_back(jnp.einsum('bshd,bthd->bhst', query_part, key_part) * causal)
    attn = jnp.einsum('bhst,bthd->bshd', scores, value_part) + jnp.einsum('bshd,bhde->bshe', query_part, kv_prefix)
    grad_scores = to_bf_and_back(jnp.einsum('bshe,bthe->bhst', grad_part, value_part) * causal)
    grad_q = jnp.einsum('bhst,bthd->bshd', grad_scores, key_part) + jnp.einsum('bshe,bhde->bshd', grad_part, kv_prefix)
    grad_k = jnp.einsum('bhst,bshd->bthd', grad_scores, query_part) + jnp.einsum('bshe,bhde->bshd', value_part, qg_suffix)
    grad_v = jnp.einsum('bhst,bshe->bthe', scores, grad_part) + jnp.einsum('bshd,bhde->bshe', key_part, qg_suffix)

    def finish(array):
        return (array * factor).reshape(SEQ_LEN, HEADS * DH).astype(jnp.bfloat16)
    return (finish(attn), finish(grad_q), finish(grad_k), finish(grad_v))
```

```python
import functools
import math

import jax
import jax.numpy as jnp
from jax import lax
from jax.experimental import pallas as pl
from jax.experimental.pallas import tpu as pltpu
from jax.sharding import PartitionSpec as P

DH = 128
F32 = jnp.float32
BF16 = jnp.bfloat16
PUT_PIECES = 3


def dot_nn(a, b):
    return lax.dot_general(a, b, (((1,), (0,)), ((), ())), preferred_element_type=F32)


def dot_nt(a, b):
    return lax.dot_general(a, b, (((1,), (1,)), ((), ())), preferred_element_type=F32)


def dot_tn(a, b):
    return lax.dot_general(a, b, (((0,), (0,)), ((), ())), preferred_element_type=F32)


def kernel(factor, q_hbm, k_hbm, v_hbm, g_hbm, one_ref, two_ref,
           ops, acc, give, mine, pre, chip, xin, yin, xsum, fin, fin_in, states,
           in_sem, pre_s, pre_r, x_s, x_r, y_s, y_r, f_s, f_r):
    me = lax.axis_index("ctx")
    core = me % 2
    xb = (me // 2) % 2
    yb = me // 4
    end = xb == yb
    mid = xb != yb
    partner = me + 1 - 2 * core
    x_dev = me + 2 - 4 * xb
    y_dev = me + 4 - 8 * yb
    tok, feat = q_hbm.shape
    half = feat // 2
    hh = half // DH

    barrier = pltpu.get_barrier_semaphore()
    for dev in (partner, x_dev, y_dev):
        pl.semaphore_signal(barrier, inc=1, device_id={"ctx": dev}, device_id_type=pl.DeviceIdType.MESH)

    cols_of = (pl.multiple_of((1 - core) * half, half), pl.multiple_of(core * half, half))
    i_k, i_v, i_q, i_g = 2 * yb, 2 * yb + 1, 2 - 2 * yb, 3 - 2 * yb

    def fetch(op, slot, ref):
        return pltpu.make_async_copy(ref.at[:, pl.ds(cols_of[slot], half)], ops.at[op, slot], in_sem.at[op, slot])

    for role in (0, 1):
        @pl.when(yb == role)
        def _():
            refs = (k_hbm, v_hbm, q_hbm, g_hbm) if role == 0 else (q_hbm, g_hbm, k_hbm, v_hbm)
            for slot in (0, 1):
                for op in range(4):
                    fetch(op, slot, refs[op]).start()

    def remote(src, dst, ss, rs, dev):
        return pltpu.make_async_remote_copy(
            src_ref=src, dst_ref=dst, send_sem=ss, recv_sem=rs,
            device_id={"ctx": dev}, device_id_type=pl.DeviceIdType.MESH)

    def pre_copy(r, h):
        return remote(give.at[r, h], pre.at[r, h], pre_s.at[r, h], pre_r.at[r, h], partner)

    def x_copy(i, src=None):
        return remote(chip.at[0, 0] if src is None else src, xin.at[i], x_s.at[i], x_r.at[i], x_dev)

    def y_copy(i, src=None):
        return remote(chip.at[0, 0] if src is None else src, yin.at[i], y_s.at[i], y_r.at[i], y_dev)

    def fin_copy(r, h):
        return remote(fin.at[r, h], fin_in.at[r, h], f_s.at[r, h], f_r.at[r, h], partner)

    def wait_ops(r, slot):
        fetch(2 * r, slot, q_hbm).wait()
        fetch(2 * r + 1, slot, q_hbm).wait()

    def head(op, slot, h):
        return ops[op, slot, :, h * DH:(h + 1) * DH]

    def local_state(r, slot, h):
        return dot_tn(head(2 * r, slot, h), head(2 * r + 1, slot, h))

    def by_place(at_end, at_mid):
        pl.when(end)(at_end)
        pl.when(mid)(at_mid)

    order = (0, 2, 1, 3)
    via_y = {2: 4, 3: 5}
    via_x = {0: 4, 1: 5}

    for r in (0, 1):
        wait_ops(r, 0)
        for h in order:
            give[r, h] = local_state(r, 0, h)
        if r == 0:
            pl.semaphore_wait(barrier, 3)
        for h in order:
            pre_copy(r, h).start()
    for r in (0, 1):
        wait_ops(r, 1)
        for h in order:
            mine[r, h] = local_state(r, 1, h)

    def adds_pre(r):
        return (core + yb + r) % 2 == 1

    def finish_state(r, h, base):
        follows = adds_pre(r)
        zero = jnp.zeros((DH, DH), F32)
        own = jnp.where(follows, pre[r, h], zero)
        other = jnp.where(follows, zero, mine[r, h])
        if base is not None:
            own, other = own + base, other + base
        states[r, 1, h] = own.astype(BF16)
        fin[r, h] = other
        fin_copy(r, h).start()

    for h in order:
        pre_copy(0, h).wait_recv()
        chip[0, h] = mine[0, h] + pre[0, h]

        def send_end():
            x_copy(h, chip.at[0, h]).start()
            y_copy(h, chip.at[0, h]).start()

        def send_mid():
            if h in via_y:
                x_copy(via_y[h], chip.at[0, h]).start()
            y_copy(h, chip.at[0, h]).start()

        by_place(send_end, send_mid)
    for h in order:
        pre_copy(1, h).wait_recv()

    def early_end():
        for h in order:
            finish_state(0, h, None)

    def early_mid():
        for h in order:
            chip[1, h] = mine[1, h] + pre[1, h]

    by_place(early_end, early_mid)

    rows = lax.broadcasted_iota(jnp.int32, (tok, tok), 0)
    columns = lax.broadcasted_iota(jnp.int32, (tok, tok), 1)

    def intra(slot, *heads):
        for h in heads:
            q, k, v, g = head(i_q, slot, h), head(i_k, slot, h), head(i_v, slot, h), head(i_g, slot, h)
            causal = columns <= rows
            sc = jnp.where(causal, dot_nt(q, k), 0.0).astype(BF16)
            ds = jnp.where(causal, dot_nt(g, v), 0.0).astype(BF16)
            acc[0, 0, slot, h] = dot_nn(sc, v)
            acc[0, 1, slot, h] = dot_nn(ds, k)
            acc[1, 0, slot, h] = dot_tn(sc, g)
            acc[1, 1, slot, h] = dot_tn(ds, q)

    def apply(r, slot, *heads):
        kind = (yb + r) % 2
        for h in heads:
            state = states[r, slot, h]
            left, right = head(2 - 2 * r, slot, h), head(3 - 2 * r, slot, h)
            at = pl.ds(pl.multiple_of(cols_of[slot] + h * DH, DH), DH)
            one_ref[kind, :, at] = ((acc[kind, 0, slot, h] + dot_nn(left, state)) * factor).astype(BF16)
            two_ref[kind, :, at] = ((acc[kind, 1, slot, h] + dot_nt(right, state)) * factor).astype(BF16)

    def take_final(r, *heads):
        for h in heads:
            fin_copy(r, h).wait_recv()
            states[r, 0, h] = fin_in[r, h].astype(BF16)
        apply(r, 0, *heads)

    def far_sum(h):
        y_copy(h).wait_recv()
        xsum[h] = chip[1, h] + yin[h]
        x_copy(h, xsum.at[h]).start()

    def relay(hx, hy):
        y_copy(hx).wait_recv()
        x_copy(via_x[hx], yin.at[hx]).start()
        x_copy(via_y[hy]).wait_recv()
        y_copy(via_y[hy], xin.at[via_y[hy]]).start()

    def near_prefix(*heads):
        for h in heads:
            x_copy(h).wait_recv()
            finish_state(0, h, xin[h])

    def end_last(*heads):
        for h in heads:
            x_copy(h).wait_recv()
            if h in via_y:
                y_copy(h).wait_recv()
            finish_state(1, h, xin[h] + yin[h])

    def mid_last(*heads):
        for h in heads:
            if h in via_y:
                y_copy(via_y[h]).wait_recv()
                finish_state(1, h, yin[h] + yin[via_y[h]])
            else:
                x_copy(via_x[h]).wait_recv()
                finish_state(1, h, yin[h] + xin[via_x[h]])

    intra(0, 0, 1)
    intra(0, 2)
    pl.when(mid)(lambda: far_sum(0))
    intra(0, 3)
    intra(1, 0)
    by_place(lambda: relay(0, 2), lambda: far_sum(2))
    intra(1, 1)
    intra(1, 2)
    by_place(lambda: relay(1, 3), lambda: far_sum(1))
    intra(1, 3)
    pl.when(mid)(lambda: near_prefix(0, 2, 1))
    pl.when(mid)(lambda: far_sum(3))
    pl.when(mid)(lambda: near_prefix(3))
    apply(0, 1, 0, 2, 1, 3)
    pl.when(end)(lambda: end_last(0, 2))
    take_final(0, 0, 2, 1, 3)
    pl.when(mid)(lambda: mid_last(0, 2))
    apply(1, 1, 0, 2)
    take_final(1, 0, 2)
    by_place(lambda: end_last(1, 3), lambda: mid_last(1, 3))
    apply(1, 1, 1, 3)
    take_final(1, 1, 3)

    for r in (0, 1):
        for h in range(hh):
            pre_copy(r, h).wait_send()
            fin_copy(r, h).wait_send()
    for i in range(hh + 2):
        x_copy(i).wait_send()
    for i in range(hh):
        y_copy(i).wait_send()

    @pl.when(end)
    def _():
        for i in range(hh, hh + 2):
            y_copy(i).wait_send()


def fused(queries, keys, values, grad_out):
    tok, feat = queries.shape
    hh = feat // DH // 2
    factor = 1.0 / math.sqrt(DH * tok * lax.axis_size("ctx"))
    state = (DH, DH)
    sem = pltpu.SemaphoreType.DMA
    return pl.pallas_call(
        functools.partial(kernel, factor),
        out_shape=[pltpu.VMEM((2, tok, feat), BF16)] * 2,
        in_specs=[pl.BlockSpec(memory_space=pltpu.HBM)] * 4,
        out_specs=[pl.BlockSpec(memory_space=pltpu.VMEM)] * 2,
        scratch_shapes=[
            pltpu.VMEM((4, 2, tok, feat // 2), BF16),
            pltpu.VMEM((2, 2, 2, hh, tok, DH), F32),
            pltpu.VMEM((2, hh) + state, F32),
            pltpu.VMEM((2, hh) + state, F32),
            pltpu.VMEM((2, hh) + state, F32),
            pltpu.VMEM((2, hh) + state, F32),
            pltpu.VMEM((hh + 2,) + state, F32),
            pltpu.VMEM((hh + 2,) + state, F32),
            pltpu.VMEM((hh,) + state, F32),
            pltpu.VMEM((2, hh) + state, F32),
            pltpu.VMEM((2, hh) + state, F32),
            pltpu.VMEM((2, 2, hh) + state, BF16),
            sem((4, 2)),
            sem((2, hh)), sem((2, hh)),
            sem((hh + 2,)), sem((hh + 2,)),
            sem((hh + 2,)), sem((hh + 2,)),
            sem((2, hh)), sem((2, hh)),
        ],
        compiler_params=pltpu.CompilerParams(
            collective_id=0, has_side_effects=True, vmem_limit_bytes=52000 * 1024),
        name="lightning",
    )(queries, keys, values, grad_out)


def put_kernel(one, two, attn, gq, gv, gk, sem):
    copies = []
    rows = attn.shape[0] // PUT_PIECES
    for i, (src, dst) in enumerate(((one.at[0], attn), (two.at[0], gq), (one.at[1], gv), (two.at[1], gk))):
        for j in range(PUT_PIECES):
            at = pl.ds(j * rows, rows)
            copies.append(pltpu.make_async_copy(src.at[at], dst.at[at], sem.at[i, j]))
    for copy in copies:
        copy.start()
    for copy in copies:
        copy.wait()


def put(results):
    shape = jax.ShapeDtypeStruct(results[0].shape[1:], BF16)
    attn, gq, gv, gk = pl.pallas_call(
        put_kernel,
        out_shape=[shape] * 4,
        in_specs=[pl.BlockSpec(memory_space=pl.ANY)] * 2,
        out_specs=[pl.BlockSpec(memory_space=pl.ANY)] * 4,
        scratch_shapes=[pltpu.SemaphoreType.DMA((4, PUT_PIECES))],
        compiler_params=pltpu.CompilerParams(vmem_limit_bytes=1024 * 1024),
        name="put",
    )(*results)
    return attn, gq, gk, gv


def carried_in(value, axis, reverse):
    devices, index = (lax.axis_size(axis), lax.axis_index(axis))
    everything = lax.all_gather(value, axis)

    def hop(k, before):
        at = devices - 1 - k if reverse else k
        reached = at > index if reverse else at < index
        return jnp.where(reached, before + everything[at], before)

    return lax.fori_loop(0, devices, hop, jnp.zeros(value.shape, value.dtype))


def general(queries, keys, values, grad_out):
    tok_rows = queries.shape[0]
    feat_width = queries.shape[1]
    heads_here = feat_width // DH
    factor = 1.0 / math.sqrt(DH * tok_rows * lax.axis_size("ctx"))
    shape_three = (tok_rows, heads_here, DH)
    query_heads = queries.reshape(shape_three)
    key_heads = keys.reshape(shape_three)
    value_heads = values.reshape(shape_three)
    grad_heads = grad_out.reshape(shape_three)
    kv_local = jnp.einsum("shd,she->hde", key_heads, value_heads, preferred_element_type=F32)
    qg_local = jnp.einsum("shd,she->hde", query_heads, grad_heads, preferred_element_type=F32)
    kv_before = carried_in(kv_local, "ctx", False).astype(BF16)
    qg_after = carried_in(qg_local, "ctx", True).astype(BF16)
    row_ids = lax.broadcasted_iota(jnp.int32, (tok_rows, tok_rows), 0)
    col_ids = lax.broadcasted_iota(jnp.int32, (tok_rows, tok_rows), 1)
    causal = (col_ids <= row_ids)[None]
    raw_scores = jnp.einsum("shd,thd->hst", query_heads, key_heads, preferred_element_type=F32)
    scores = jnp.where(causal, raw_scores, 0.0).astype(BF16)
    attn = jnp.einsum("hst,thd->shd", scores, value_heads, preferred_element_type=F32)
    attn = attn + jnp.einsum("shd,hde->she", query_heads, kv_before, preferred_element_type=F32)
    raw_grad = jnp.einsum("she,the->hst", grad_heads, value_heads, preferred_element_type=F32)
    grad_scores = jnp.where(causal, raw_grad, 0.0).astype(BF16)
    grad_q = jnp.einsum("hst,thd->shd", grad_scores, key_heads, preferred_element_type=F32)
    grad_q = grad_q + jnp.einsum("she,hde->shd", grad_heads, kv_before, preferred_element_type=F32)
    grad_k = jnp.einsum("hst,shd->thd", grad_scores, query_heads, preferred_element_type=F32)
    grad_k = grad_k + jnp.einsum("she,hde->shd", value_heads, qg_after, preferred_element_type=F32)
    grad_v = jnp.einsum("hst,she->the", scores, grad_heads, preferred_element_type=F32)
    grad_v = grad_v + jnp.einsum("shd,hde->she", key_heads, qg_after, preferred_element_type=F32)

    def finish(array):
        return (array * factor).reshape(tok_rows, feat_width).astype(BF16)

    return (finish(attn), finish(grad_q), finish(grad_k), finish(grad_v))


def local(queries, keys, values, grad_out):
    if lax.axis_size("ctx") == 8 and queries.shape[1] == 8 * DH:
        return put(fused(queries, keys, values, grad_out))
    return general(queries, keys, values, grad_out)


def solution(mesh):
    spec = P(("seq", "ctx"), "head")
    return jax.shard_map(local, mesh=mesh, in_specs=(spec,) * 4, out_specs=(spec,) * 4, check_vma=False)
```

```python
import functools
import math

import jax
import jax.numpy as jnp
from jax import lax
from jax.experimental import pallas as pl
from jax.experimental.pallas import tpu as pltpu
from jax.sharding import PartitionSpec as P

DH = 128
F32 = jnp.float32
BF16 = jnp.bfloat16
PUT_PIECES = 3


def dot_nn(a, b):
    return lax.dot_general(a, b, (((1,), (0,)), ((), ())), preferred_element_type=F32)


def dot_nt(a, b):
    return lax.dot_general(a, b, (((1,), (1,)), ((), ())), preferred_element_type=F32)


def dot_tn(a, b):
    return lax.dot_general(a, b, (((0,), (0,)), ((), ())), preferred_element_type=F32)


def kernel(factor, q_hbm, k_hbm, v_hbm, g_hbm, one_ref, two_ref,
           ops, acc, give, mine, pre, chip, xin, yin, sums, fin, fin_in, states,
           in_sem, pre_s, pre_r, x_s, x_r, y_s, y_r, f_s, f_r):
    me = lax.axis_index("ctx")
    core = me % 2
    xb = (me // 2) % 2
    yb = me // 4
    end = xb == yb
    mid = xb != yb
    partner = me + 1 - 2 * core
    x_dev = me + 2 - 4 * xb
    y_dev = me + 4 - 8 * yb
    tok, feat = q_hbm.shape
    half = feat // 2
    hh = half // DH

    barrier = pltpu.get_barrier_semaphore()
    for dev in (partner, x_dev, y_dev):
        pl.semaphore_signal(barrier, inc=1, device_id={"ctx": dev}, device_id_type=pl.DeviceIdType.MESH)

    cols_of = (pl.multiple_of((1 - core) * half, half), pl.multiple_of(core * half, half))
    i_k, i_v, i_q, i_g = 2 * yb, 2 * yb + 1, 2 - 2 * yb, 3 - 2 * yb

    def fetch(op, slot, ref):
        return pltpu.make_async_copy(ref.at[:, pl.ds(cols_of[slot], half)], ops.at[op, slot], in_sem.at[op, slot])

    for role in (0, 1):
        @pl.when(yb == role)
        def _():
            refs = (k_hbm, v_hbm, q_hbm, g_hbm) if role == 0 else (q_hbm, g_hbm, k_hbm, v_hbm)
            for slot in (0, 1):
                for op in range(4):
                    fetch(op, slot, refs[op]).start()

    def remote(src, dst, ss, rs, dev):
        return pltpu.make_async_remote_copy(
            src_ref=src, dst_ref=dst, send_sem=ss, recv_sem=rs,
            device_id={"ctx": dev}, device_id_type=pl.DeviceIdType.MESH)

    def pre_copy(r, h):
        return remote(give.at[r, h], pre.at[r, h], pre_s.at[r, h], pre_r.at[r, h], partner)

    def x_copy(i, src=None):
        return remote(chip.at[0, 0] if src is None else src, xin.at[i], x_s.at[i], x_r.at[i], x_dev)

    def y_copy(i, src=None):
        return remote(chip.at[0, 0] if src is None else src, yin.at[i], y_s.at[i], y_r.at[i], y_dev)

    def fin_copy(r, h):
        return remote(fin.at[r, h], fin_in.at[r, h], f_s.at[r, h], f_r.at[r, h], partner)

    def wait_ops(r, slot):
        fetch(2 * r, slot, q_hbm).wait()
        fetch(2 * r + 1, slot, q_hbm).wait()

    def head(op, slot, h):
        return ops[op, slot, :, h * DH:(h + 1) * DH]

    def local_state(r, slot, h):
        return dot_tn(head(2 * r, slot, h), head(2 * r + 1, slot, h))

    def by_place(at_end, at_mid):
        pl.when(end)(at_end)
        pl.when(mid)(at_mid)

    order = (0, 2, 1, 3)

    for r in (0, 1):
        wait_ops(r, 0)
        for h in order:
            give[r, h] = local_state(r, 0, h)
        if r == 0:
            pl.semaphore_wait(barrier, 3)
        for h in order:
            pre_copy(r, h).start()
    for r in (0, 1):
        wait_ops(r, 1)
        for h in order:
            mine[r, h] = local_state(r, 1, h)

    def adds_pre(r):
        return (core + yb + r) % 2 == 1

    def finish_state(r, h, base):
        follows = adds_pre(r)
        zero = jnp.zeros((DH, DH), F32)
        own = jnp.where(follows, pre[r, h], zero)
        other = jnp.where(follows, zero, mine[r, h])
        if base is not None:
            own, other = own + base, other + base
        states[r, 1, h] = own.astype(BF16)
        fin[r, h] = other
        fin_copy(r, h).start()

    for h in order:
        pre_copy(0, h).wait_recv()
        chip[0, h] = mine[0, h] + pre[0, h]

        def send_end():
            (x_copy if h >= 2 else y_copy)(h, chip.at[0, h]).start()

        def send_mid():
            if h >= 2:
                x_copy(h + 2, chip.at[0, h]).start()
            else:
                y_copy(h, chip.at[0, h]).start()

        by_place(send_end, send_mid)

    @pl.when(end)
    def _():
        for h in (0, 1):
            x_copy(h, chip.at[0, h]).start()
        for h in (2, 3):
            y_copy(h, chip.at[0, h]).start()

    for h in (2, 3, 0, 1):
        pre_copy(1, h).wait_recv()

        def far_mid():
            chip[1, h] = mine[1, h] + pre[1, h]
            if h >= 2:
                x_copy(h, chip.at[1, h]).start()

        pl.when(mid)(far_mid)

    @pl.when(end)
    def _():
        for h in range(hh):
            finish_state(0, h, None)

    rows = lax.broadcasted_iota(jnp.int32, (tok, tok), 0)
    columns = lax.broadcasted_iota(jnp.int32, (tok, tok), 1)

    def intra(slot, *heads):
        for h in heads:
            q, k, v, g = head(i_q, slot, h), head(i_k, slot, h), head(i_v, slot, h), head(i_g, slot, h)
            causal = columns <= rows
            sc = jnp.where(causal, dot_nt(q, k), 0.0).astype(BF16)
            ds = jnp.where(causal, dot_nt(g, v), 0.0).astype(BF16)
            acc[0, 0, slot, h] = dot_nn(sc, v)
            acc[0, 1, slot, h] = dot_nn(ds, k)
            acc[1, 0, slot, h] = dot_tn(sc, g)
            acc[1, 1, slot, h] = dot_tn(ds, q)

    def apply(r, slot, *heads):
        kind = (yb + r) % 2
        for h in heads:
            state = states[r, slot, h]
            left, right = head(2 - 2 * r, slot, h), head(3 - 2 * r, slot, h)
            at = pl.ds(pl.multiple_of(cols_of[slot] + h * DH, DH), DH)
            one_ref[kind, :, at] = ((acc[kind, 0, slot, h] + dot_nn(left, state)) * factor).astype(BF16)
            two_ref[kind, :, at] = ((acc[kind, 1, slot, h] + dot_nt(right, state)) * factor).astype(BF16)

    def take_final(r, *heads):
        for h in heads:
            fin_copy(r, h).wait_recv()
            states[r, 0, h] = fin_in[r, h].astype(BF16)
        apply(r, 0, *heads)

    def mid_sums(hx, hy):
        x_copy(hx).wait_recv()
        sums[hx] = chip[0, hx] + xin[hx]
        y_copy(hx, sums.at[hx]).start()
        y_copy(hy).wait_recv()
        sums[hy] = chip[1, hy] + yin[hy]
        x_copy(hy, sums.at[hy]).start()

    def relay(hy, hx):
        y_copy(hy).wait_recv()
        x_copy(4 + hy, yin.at[hy]).start()
        x_copy(2 + hx).wait_recv()
        y_copy(2 + hx, xin.at[2 + hx]).start()

    def near_prefix(*heads):
        for h in heads:
            if h < 2:
                x_copy(h).wait_recv()
            finish_state(0, h, xin[h])

    def end_last(*heads):
        for h in heads:
            x_copy(h).wait_recv()
            if h >= 2:
                y_copy(h).wait_recv()
            finish_state(1, h, xin[h] + yin[h])

    def mid_last(*heads):
        for h in heads:
            if h < 2:
                x_copy(4 + h).wait_recv()
                finish_state(1, h, yin[h] + xin[4 + h])
            else:
                y_copy(h).wait_recv()
                y_copy(2 + h).wait_recv()
                finish_state(1, h, yin[h] + yin[2 + h])

    def end_tail():
        apply(0, 1, *order)
        take_final(0, *order)
        end_last(2, 3)
        apply(1, 1, 2, 3)
        end_last(0)
        take_final(1, 2, 3)
        apply(1, 1, 0)
        end_last(1)
        apply(1, 1, 1)
        take_final(1, 0, 1)

    def mid_tail():
        near_prefix(1)
        apply(0, 1, *order)
        take_final(0, *order)
        mid_last(0, 2)
        apply(1, 1, 0, 2)
        take_final(1, 0, 2)
        mid_last(1, 3)
        apply(1, 1, 1, 3)
        take_final(1, 1, 3)

    intra(0, 0, 1)
    intra(0, 2)
    by_place(lambda: relay(0, 2), lambda: mid_sums(2, 0))
    intra(0, 3)
    pl.when(mid)(lambda: mid_sums(3, 1))
    intra(1, 0)
    by_place(lambda: relay(1, 3), lambda: near_prefix(2, 3))
    intra(1, 1)
    pl.when(mid)(lambda: near_prefix(0))
    intra(1, 2, 3)
    by_place(end_tail, mid_tail)

    for r in (0, 1):
        for h in range(hh):
            pre_copy(r, h).wait_send()
            fin_copy(r, h).wait_send()
    for i in range(hh + 2):
        x_copy(i).wait_send()
    for i in range(hh):
        y_copy(i).wait_send()

    @pl.when(end)
    def _():
        for i in range(hh, hh + 2):
            y_copy(i).wait_send()


def fused(queries, keys, values, grad_out):
    tok, feat = queries.shape
    hh = feat // DH // 2
    factor = 1.0 / math.sqrt(DH * tok * lax.axis_size("ctx"))
    state = (DH, DH)
    sem = pltpu.SemaphoreType.DMA
    return pl.pallas_call(
        functools.partial(kernel, factor),
        out_shape=[pltpu.VMEM((2, tok, feat), BF16)] * 2,
        in_specs=[pl.BlockSpec(memory_space=pltpu.HBM)] * 4,
        out_specs=[pl.BlockSpec(memory_space=pltpu.VMEM)] * 2,
        scratch_shapes=[
            pltpu.VMEM((4, 2, tok, feat // 2), BF16),
            pltpu.VMEM((2, 2, 2, hh, tok, DH), F32),
            pltpu.VMEM((2, hh) + state, F32),
            pltpu.VMEM((2, hh) + state, F32),
            pltpu.VMEM((2, hh) + state, F32),
            pltpu.VMEM((2, hh) + state, F32),
            pltpu.VMEM((hh + 2,) + state, F32),
            pltpu.VMEM((hh + 2,) + state, F32),
            pltpu.VMEM((hh,) + state, F32),
            pltpu.VMEM((2, hh) + state, F32),
            pltpu.VMEM((2, hh) + state, F32),
            pltpu.VMEM((2, 2, hh) + state, BF16),
            sem((4, 2)),
            sem((2, hh)), sem((2, hh)),
            sem((hh + 2,)), sem((hh + 2,)),
            sem((hh + 2,)), sem((hh + 2,)),
            sem((2, hh)), sem((2, hh)),
        ],
        compiler_params=pltpu.CompilerParams(
            collective_id=0, has_side_effects=True, vmem_limit_bytes=52000 * 1024),
        name="lightning",
    )(queries, keys, values, grad_out)


def put_kernel(one, two, attn, gq, gv, gk, sem):
    copies = []
    rows = attn.shape[0] // PUT_PIECES
    for i, (src, dst) in enumerate(((one.at[0], attn), (two.at[0], gq), (one.at[1], gv), (two.at[1], gk))):
        for j in range(PUT_PIECES):
            at = pl.ds(j * rows, rows)
            copies.append(pltpu.make_async_copy(src.at[at], dst.at[at], sem.at[i, j]))
    for copy in copies:
        copy.start()
    for copy in copies:
        copy.wait()


def put(results):
    shape = jax.ShapeDtypeStruct(results[0].shape[1:], BF16)
    attn, gq, gv, gk = pl.pallas_call(
        put_kernel,
        out_shape=[shape] * 4,
        in_specs=[pl.BlockSpec(memory_space=pl.ANY)] * 2,
        out_specs=[pl.BlockSpec(memory_space=pl.ANY)] * 4,
        scratch_shapes=[pltpu.SemaphoreType.DMA((4, PUT_PIECES))],
        compiler_params=pltpu.CompilerParams(vmem_limit_bytes=1024 * 1024),
        name="put",
    )(*results)
    return attn, gq, gk, gv


def carried_in(value, axis, reverse):
    devices, index = (lax.axis_size(axis), lax.axis_index(axis))
    everything = lax.all_gather(value, axis)

    def hop(k, before):
        at = devices - 1 - k if reverse else k
        reached = at > index if reverse else at < index
        return jnp.where(reached, before + everything[at], before)

    return lax.fori_loop(0, devices, hop, jnp.zeros(value.shape, value.dtype))


def general(queries, keys, values, grad_out):
    tok_rows = queries.shape[0]
    feat_width = queries.shape[1]
    heads_here = feat_width // DH
    factor = 1.0 / math.sqrt(DH * tok_rows * lax.axis_size("ctx"))
    shape_three = (tok_rows, heads_here, DH)
    query_heads = queries.reshape(shape_three)
    key_heads = keys.reshape(shape_three)
    value_heads = values.reshape(shape_three)
    grad_heads = grad_out.reshape(shape_three)
    kv_local = jnp.einsum("shd,she->hde", key_heads, value_heads, preferred_element_type=F32)
    qg_local = jnp.einsum("shd,she->hde", query_heads, grad_heads, preferred_element_type=F32)
    kv_before = carried_in(kv_local, "ctx", False).astype(BF16)
    qg_after = carried_in(qg_local, "ctx", True).astype(BF16)
    row_ids = lax.broadcasted_iota(jnp.int32, (tok_rows, tok_rows), 0)
    col_ids = lax.broadcasted_iota(jnp.int32, (tok_rows, tok_rows), 1)
    causal = (col_ids <= row_ids)[None]
    raw_scores = jnp.einsum("shd,thd->hst", query_heads, key_heads, preferred_element_type=F32)
    scores = jnp.where(causal, raw_scores, 0.0).astype(BF16)
    attn = jnp.einsum("hst,thd->shd", scores, value_heads, preferred_element_type=F32)
    attn = attn + jnp.einsum("shd,hde->she", query_heads, kv_before, preferred_element_type=F32)
    raw_grad = jnp.einsum("she,the->hst", grad_heads, value_heads, preferred_element_type=F32)
    grad_scores = jnp.where(causal, raw_grad, 0.0).astype(BF16)
    grad_q = jnp.einsum("hst,thd->shd", grad_scores, key_heads, preferred_element_type=F32)
    grad_q = grad_q + jnp.einsum("she,hde->shd", grad_heads, kv_before, preferred_element_type=F32)
    grad_k = jnp.einsum("hst,shd->thd", grad_scores, query_heads, preferred_element_type=F32)
    grad_k = grad_k + jnp.einsum("she,hde->shd", value_heads, qg_after, preferred_element_type=F32)
    grad_v = jnp.einsum("hst,she->the", scores, grad_heads, preferred_element_type=F32)
    grad_v = grad_v + jnp.einsum("shd,hde->she", key_heads, qg_after, preferred_element_type=F32)

    def finish(array):
        return (array * factor).reshape(tok_rows, feat_width).astype(BF16)

    return (finish(attn), finish(grad_q), finish(grad_k), finish(grad_v))


def local(queries, keys, values, grad_out):
    if lax.axis_size("ctx") == 8 and queries.shape[1] == 8 * DH:
        return put(fused(queries, keys, values, grad_out))
    return general(queries, keys, values, grad_out)


def solution(mesh):
    spec = P(("seq", "ctx"), "head")
    return jax.shard_map(local, mesh=mesh, in_specs=(spec,) * 4, out_specs=(spec,) * 4, check_vma=False)
```

```python
import functools
import math

import jax
import jax.numpy as jnp
from jax import lax
from jax.experimental import pallas as pl
from jax.experimental.pallas import tpu as pltpu
from jax.sharding import PartitionSpec as P

DH = 128
F32 = jnp.float32
BF16 = jnp.bfloat16


def dot_nn(a, b):
    return lax.dot_general(a, b, (((1,), (0,)), ((), ())), preferred_element_type=F32)


def dot_nt(a, b):
    return lax.dot_general(a, b, (((1,), (1,)), ((), ())), preferred_element_type=F32)


def dot_tn(a, b):
    return lax.dot_general(a, b, (((0,), (0,)), ((), ())), preferred_element_type=F32)


def kernel(factor, q_hbm, k_hbm, v_hbm, g_hbm, one_ref, two_ref,
           ops, acc, give, mine, pre, chip, xin, yin, sums, fin, fin_in, states,
           in_sem, pre_s, pre_r, x_s, x_r, y_s, y_r, f_s, f_r):
    me = lax.axis_index("ctx")
    core = me % 2
    xb = (me // 2) % 2
    yb = me // 4
    end = xb == yb
    mid = xb != yb
    partner = me + 1 - 2 * core
    x_dev = me + 2 - 4 * xb
    y_dev = me + 4 - 8 * yb
    tok, feat = q_hbm.shape
    half = feat // 2
    hh = half // DH

    barrier = pltpu.get_barrier_semaphore()
    for dev in (partner, x_dev, y_dev):
        pl.semaphore_signal(barrier, inc=1, device_id={"ctx": dev}, device_id_type=pl.DeviceIdType.MESH)

    cols_of = (pl.multiple_of((1 - core) * half, half), pl.multiple_of(core * half, half))
    i_k, i_v, i_q, i_g = 2 * yb, 2 * yb + 1, 2 - 2 * yb, 3 - 2 * yb

    def fetch(op, slot, ref):
        return pltpu.make_async_copy(ref.at[:, pl.ds(cols_of[slot], half)], ops.at[op, slot], in_sem.at[op // 2, slot])

    for role in (0, 1):
        @pl.when(yb == role)
        def _():
            refs = (k_hbm, v_hbm, q_hbm, g_hbm) if role == 0 else (q_hbm, g_hbm, k_hbm, v_hbm)
            for slot in (0, 1):
                for op in range(4):
                    fetch(op, slot, refs[op]).start()

    def remote(src, dst, ss, rs, dev):
        return pltpu.make_async_remote_copy(
            src_ref=src, dst_ref=dst, send_sem=ss, recv_sem=rs,
            device_id={"ctx": dev}, device_id_type=pl.DeviceIdType.MESH)

    def pre_copy(r, h):
        return remote(give.at[r, h], pre.at[r, h], pre_s, pre_r.at[r, h], partner)

    def x_copy(i, src=None):
        return remote(chip.at[0, 0] if src is None else src, xin.at[i], x_s, x_r.at[i], x_dev)

    def y_copy(i, src=None):
        return remote(chip.at[0, 0] if src is None else src, yin.at[i], y_s, y_r.at[i], y_dev)

    def fin_copy(r, h):
        return remote(fin.at[r, h], fin_in.at[r, h], f_s, f_r.at[r, h], partner)

    def wait_ops(r, slot):
        both = ops.at[2 * r:2 * r + 2, slot]
        pltpu.make_async_copy(both, both, in_sem.at[r, slot]).wait()

    def head(op, slot, h):
        return ops[op, slot, :, h * DH:(h + 1) * DH]

    def local_state(r, slot, h):
        return dot_tn(head(2 * r, slot, h), head(2 * r + 1, slot, h))

    def by_place(at_end, at_mid):
        pl.when(end)(at_end)
        pl.when(mid)(at_mid)

    order = (0, 2, 1, 3)

    for r in (0, 1):
        wait_ops(r, 0)
        for h in order:
            give[r, h] = local_state(r, 0, h)
        if r == 0:
            pl.semaphore_wait(barrier, 3)
        for h in order:
            pre_copy(r, h).start()
    for r in (0, 1):
        wait_ops(r, 1)
        for h in order:
            mine[r, h] = local_state(r, 1, h)

    def adds_pre(r):
        return (core + yb + r) % 2 == 1

    def finish_state(r, h, base):
        follows = adds_pre(r)
        zero = jnp.zeros((DH, DH), F32)
        own = jnp.where(follows, pre[r, h], zero)
        other = jnp.where(follows, zero, mine[r, h])
        if base is not None:
            own, other = own + base, other + base
        states[r, 1, h] = own.astype(BF16)
        fin[r, h] = other
        fin_copy(r, h).start()

    for h in order:
        pre_copy(0, h).wait_recv()
        chip[0, h] = mine[0, h] + pre[0, h]

        def send_end():
            (x_copy if h >= 2 else y_copy)(h, chip.at[0, h]).start()

        def send_mid():
            if h >= 2:
                x_copy(h + 2, chip.at[0, h]).start()
            else:
                y_copy(h, chip.at[0, h]).start()

        by_place(send_end, send_mid)

    @pl.when(end)
    def _():
        for h in (0, 1):
            x_copy(h, chip.at[0, h]).start()
        for h in (2, 3):
            y_copy(h, chip.at[0, h]).start()

    for h in (2, 3, 0, 1):
        pre_copy(1, h).wait_recv()

        def far_mid():
            chip[1, h] = mine[1, h] + pre[1, h]
            if h >= 2:
                x_copy(h, chip.at[1, h]).start()

        pl.when(mid)(far_mid)

    @pl.when(end)
    def _():
        for h in range(hh):
            finish_state(0, h, None)

    rows = lax.broadcasted_iota(jnp.int32, (tok, tok), 0)
    columns = lax.broadcasted_iota(jnp.int32, (tok, tok), 1)

    def intra(slot, *heads):
        for h in heads:
            q, k, v, g = head(i_q, slot, h), head(i_k, slot, h), head(i_v, slot, h), head(i_g, slot, h)
            causal = columns <= rows
            sc = jnp.where(causal, dot_nt(q, k), 0.0).astype(BF16)
            ds = jnp.where(causal, dot_nt(g, v), 0.0).astype(BF16)
            acc[0, 0, slot, h] = dot_nn(sc, v)
            acc[0, 1, slot, h] = dot_nn(ds, k)
            acc[1, 0, slot, h] = dot_tn(sc, g)
            acc[1, 1, slot, h] = dot_tn(ds, q)

    def apply(r, slot, *heads):
        kind = (yb + r) % 2
        for h in heads:
            state = states[r, slot, h]
            left, right = head(2 - 2 * r, slot, h), head(3 - 2 * r, slot, h)
            at = pl.ds(pl.multiple_of(cols_of[slot] + h * DH, DH), DH)
            one_ref[kind, :, at] = ((acc[kind, 0, slot, h] + dot_nn(left, state)) * factor).astype(BF16)
            two_ref[kind, :, at] = ((acc[kind, 1, slot, h] + dot_nt(right, state)) * factor).astype(BF16)

    def take_final(r, *heads):
        for h in heads:
            fin_copy(r, h).wait_recv()
            states[r, 0, h] = fin_in[r, h].astype(BF16)
        apply(r, 0, *heads)

    def mid_sums(hx, hy):
        x_copy(hx).wait_recv()
        sums[hx] = chip[0, hx] + xin[hx]
        y_copy(hx, sums.at[hx]).start()
        y_copy(hy).wait_recv()
        sums[hy] = chip[1, hy] + yin[hy]
        x_copy(hy, sums.at[hy]).start()

    def relay(hy, hx):
        y_copy(hy).wait_recv()
        x_copy(4 + hy, yin.at[hy]).start()
        x_copy(2 + hx).wait_recv()
        y_copy(2 + hx, xin.at[2 + hx]).start()

    def near_prefix(*heads):
        for h in heads:
            if h < 2:
                x_copy(h).wait_recv()
            finish_state(0, h, xin[h])

    def end_last(*heads):
        for h in heads:
            x_copy(h).wait_recv()
            if h >= 2:
                y_copy(h).wait_recv()
            finish_state(1, h, xin[h] + yin[h])

    def mid_last(*heads):
        for h in heads:
            if h < 2:
                x_copy(4 + h).wait_recv()
                finish_state(1, h, yin[h] + xin[4 + h])
            else:
                y_copy(h).wait_recv()
                y_copy(2 + h).wait_recv()
                finish_state(1, h, yin[h] + yin[2 + h])

    def end_tail():
        apply(0, 1, *order)
        take_final(0, *order)
        end_last(2, 3)
        apply(1, 1, 2, 3)
        end_last(0)
        take_final(1, 2, 3)
        apply(1, 1, 0)
        end_last(1)
        apply(1, 1, 1)
        take_final(1, 0, 1)

    def mid_tail():
        near_prefix(1)
        apply(0, 1, *order)
        mid_last(0, 2)
        apply(1, 1, 0, 2)
        take_final(0, *order)
        mid_last(1, 3)
        apply(1, 1, 1, 3)
        take_final(1, 0, 2)
        take_final(1, 1, 3)

    intra(0, 0, 1)
    intra(0, 2)
    by_place(lambda: relay(0, 2), lambda: mid_sums(2, 0))
    intra(0, 3)
    pl.when(mid)(lambda: mid_sums(3, 1))
    intra(1, 0)
    by_place(lambda: relay(1, 3), lambda: near_prefix(2, 3))
    intra(1, 1)
    pl.when(mid)(lambda: near_prefix(0))
    intra(1, 2, 3)
    by_place(end_tail, mid_tail)

    remote(give, pre, pre_s, pre_r.at[0, 0], partner).wait_send()
    remote(fin, fin_in, f_s, f_r.at[0, 0], partner).wait_send()
    remote(xin, xin, x_s, x_r.at[0], x_dev).wait_send()

    def sent_y(count):
        part = yin.at[0:count]
        remote(part, part, y_s, y_r.at[0], y_dev).wait_send()

    by_place(lambda: sent_y(hh + 2), lambda: sent_y(hh))


def fused(queries, keys, values, grad_out):
    tok, feat = queries.shape
    hh = feat // DH // 2
    factor = 1.0 / math.sqrt(DH * tok * lax.axis_size("ctx"))
    state = (DH, DH)
    sem = pltpu.SemaphoreType.DMA
    return pl.pallas_call(
        functools.partial(kernel, factor),
        out_shape=[pltpu.VMEM((2, tok, feat), BF16)] * 2,
        in_specs=[pl.BlockSpec(memory_space=pltpu.HBM)] * 4,
        out_specs=[pl.BlockSpec(memory_space=pltpu.VMEM)] * 2,
        scratch_shapes=[
            pltpu.VMEM((4, 2, tok, feat // 2), BF16),
            pltpu.VMEM((2, 2, 2, hh, tok, DH), F32),
            pltpu.VMEM((2, hh) + state, F32),
            pltpu.VMEM((2, hh) + state, F32),
            pltpu.VMEM((2, hh) + state, F32),
            pltpu.VMEM((2, hh) + state, F32),
            pltpu.VMEM((hh + 2,) + state, F32),
            pltpu.VMEM((hh + 2,) + state, F32),
            pltpu.VMEM((hh,) + state, F32),
            pltpu.VMEM((2, hh) + state, F32),
            pltpu.VMEM((2, hh) + state, F32),
            pltpu.VMEM((2, 2, hh) + state, BF16),
            sem((2, 2)),
            sem, sem((2, hh)),
            sem, sem((hh + 2,)),
            sem, sem((hh + 2,)),
            sem, sem((2, hh)),
        ],
        compiler_params=pltpu.CompilerParams(
            collective_id=0, has_side_effects=True, vmem_limit_bytes=52000 * 1024),
        name="lightning",
    )(queries, keys, values, grad_out)


def put_kernel(one, two, attn, gq, gv, gk, sem):
    copies = [
        pltpu.make_async_copy(src, dst, sem.at[i])
        for i, (src, dst) in enumerate(((one.at[0], attn), (two.at[0], gq), (one.at[1], gv), (two.at[1], gk)))]
    for copy in copies:
        copy.start()
    for copy in copies:
        copy.wait()


def put(results):
    shape = jax.ShapeDtypeStruct(results[0].shape[1:], BF16)
    attn, gq, gv, gk = pl.pallas_call(
        put_kernel,
        out_shape=[shape] * 4,
        in_specs=[pl.BlockSpec(memory_space=pl.ANY)] * 2,
        out_specs=[pl.BlockSpec(memory_space=pl.ANY)] * 4,
        scratch_shapes=[pltpu.SemaphoreType.DMA((4,))],
        compiler_params=pltpu.CompilerParams(vmem_limit_bytes=1024 * 1024),
        name="put",
    )(*results)
    return attn, gq, gk, gv


def carried_in(value, axis, reverse):
    devices, index = (lax.axis_size(axis), lax.axis_index(axis))
    everything = lax.all_gather(value, axis)

    def hop(k, before):
        at = devices - 1 - k if reverse else k
        reached = at > index if reverse else at < index
        return jnp.where(reached, before + everything[at], before)

    return lax.fori_loop(0, devices, hop, jnp.zeros(value.shape, value.dtype))


def general(queries, keys, values, grad_out):
    tok_rows = queries.shape[0]
    feat_width = queries.shape[1]
    heads_here = feat_width // DH
    factor = 1.0 / math.sqrt(DH * tok_rows * lax.axis_size("ctx"))
    shape_three = (tok_rows, heads_here, DH)
    query_heads = queries.reshape(shape_three)
    key_heads = keys.reshape(shape_three)
    value_heads = values.reshape(shape_three)
    grad_heads = grad_out.reshape(shape_three)
    kv_local = jnp.einsum("shd,she->hde", key_heads, value_heads, preferred_element_type=F32)
    qg_local = jnp.einsum("shd,she->hde", query_heads, grad_heads, preferred_element_type=F32)
    kv_before = carried_in(kv_local, "ctx", False).astype(BF16)
    qg_after = carried_in(qg_local, "ctx", True).astype(BF16)
    row_ids = lax.broadcasted_iota(jnp.int32, (tok_rows, tok_rows), 0)
    col_ids = lax.broadcasted_iota(jnp.int32, (tok_rows, tok_rows), 1)
    causal = (col_ids <= row_ids)[None]
    raw_scores = jnp.einsum("shd,thd->hst", query_heads, key_heads, preferred_element_type=F32)
    scores = jnp.where(causal, raw_scores, 0.0).astype(BF16)
    attn = jnp.einsum("hst,thd->shd", scores, value_heads, preferred_element_type=F32)
    attn = attn + jnp.einsum("shd,hde->she", query_heads, kv_before, preferred_element_type=F32)
    raw_grad = jnp.einsum("she,the->hst", grad_heads, value_heads, preferred_element_type=F32)
    grad_scores = jnp.where(causal, raw_grad, 0.0).astype(BF16)
    grad_q = jnp.einsum("hst,thd->shd", grad_scores, key_heads, preferred_element_type=F32)
    grad_q = grad_q + jnp.einsum("she,hde->shd", grad_heads, kv_before, preferred_element_type=F32)
    grad_k = jnp.einsum("hst,shd->thd", grad_scores, query_heads, preferred_element_type=F32)
    grad_k = grad_k + jnp.einsum("she,hde->shd", value_heads, qg_after, preferred_element_type=F32)
    grad_v = jnp.einsum("hst,she->the", scores, grad_heads, preferred_element_type=F32)
    grad_v = grad_v + jnp.einsum("shd,hde->she", key_heads, qg_after, preferred_element_type=F32)

    def finish(array):
        return (array * factor).reshape(tok_rows, feat_width).astype(BF16)

    return (finish(attn), finish(grad_q), finish(grad_k), finish(grad_v))


def local(queries, keys, values, grad_out):
    if lax.axis_size("ctx") == 8 and queries.shape[1] == 8 * DH:
        return put(fused(queries, keys, values, grad_out))
    return general(queries, keys, values, grad_out)


def solution(mesh):
    spec = P(("seq", "ctx"), "head")
    return jax.shard_map(local, mesh=mesh, in_specs=(spec,) * 4, out_specs=(spec,) * 4, check_vma=False)
```
